32 devices in a mesh: grp: 2 (over y), smp: 8 (over z, x), feat: 2 (over core).
Axes of the slice: x: 2, y: 2, z: 4, core: 2. Of those that a mesh axis runs over, the one named last changes fastest.
Arguments:
- coal_size: int32 [1024], P(('grp', 'smp')), parts along dimension 0, may hold values from 1536 to 2559
- coal_step: int32 [1024], P(('grp', 'smp')), parts along dimension 0, may hold values from 0 to 2047
- coal_shift: int32 [1024], P(('grp', 'smp')), parts along dimension 0, may hold values from 0 to 4095
- outputs_y: float32 [1024, 32], P(('grp', 'smp')), parts along dimension 0, may hold values from -6 to 6
Outputs:
- attributions: float32 [8192, 32], P(('grp', 'smp', 'feat')), parts along dimension 0
- residual: float32 [8192, 32], P(('grp', 'smp', 'feat')), parts along dimension 0
The draws below stay inside these ranges and needn't reach their ends.
There are 2 independent parts, one for each index of `grp`. The reference program is written for one: setup_inputs(seed, part) draws one part's arguments, and reference() takes and returns one part's arrays. A program takes and returns all parts, laid end to end along the dimension named above; each array names one. Nothing has to cross between parts.
All inputs are finite; a program needn't handle non-finite values.
Results may differ from the reference program's by a relative error of at most 0.0003.
Values sent between devices are 32-bit elements; how exact they have to be, the bound alone decides.
A program may use at most 64 MiB of HBM per device.

```python
import jax
import jax.numpy as jnp
from jax import lax

F = 4096
R = 32
ITERS = 2
SAMPLES = 512


def with_ends(array, own_key, smallest, high):
    spot = [jax.random.randint(jax.random.fold_in(own_key, axis), (), 0, length) for axis, length in enumerate(array.shape)]
    widest = array.shape.index(max(array.shape))
    neighbour = spot[:widest] + [(spot[widest] + 1) % array.shape[widest]] + spot[widest + 1:]
    return array.at[tuple(spot)].set(smallest).at[tuple(neighbour)].set(high)


def block_scale(stream_key, dims, cuts, low, largest):
    gain = 1.0
    for axis_at, parts in cuts:
        heights = jax.random.uniform(jax.random.fold_in(jax.random.fold_in(stream_key, 6), axis_at), (parts,), jnp.float32, low / len(cuts), largest / len(cuts))
        gain = gain * jnp.repeat(jnp.exp(heights), dims[axis_at] // parts).reshape((-1,) + (1,) * (len(dims) - 1 - axis_at))
    return gain


def scatter_about(own_key, extent, spread, reach, cuts=(), held_as=jnp.bfloat16):
    drawn = spread * jax.random.normal(own_key, extent, jnp.float32)
    if cuts:
        drawn = drawn * block_scale(own_key, extent, cuts, -0.22, 0.18)
    return jnp.clip(drawn, -reach, reach).astype(held_as)


def setup_inputs(seed: int = 0, part: int = 0) -> dict:
    keys = jax.random.split(jax.random.key(seed), 5)
    part_keys = jax.random.split(jax.random.fold_in(keys[4], part), 5)
    return {
        "coal_size": with_ends(jax.random.randint(part_keys[0], (SAMPLES,), 3 * F // 8, 5 * F // 8), jax.random.fold_in(part_keys[0], 1), 3 * F // 8, (5 * F // 8) - 1).astype(jnp.int32),
        "coal_step": with_ends(jax.random.randint(part_keys[1], (SAMPLES,), 0, F // 2), jax.random.fold_in(part_keys[1], 1), 0, (F // 2) - 1).astype(jnp.int32),
        "coal_shift": with_ends(jax.random.randint(part_keys[2], (SAMPLES,), 0, F), jax.random.fold_in(part_keys[2], 1), 0, F - 1).astype(jnp.int32),
        "outputs_y": scatter_about(part_keys[3], (SAMPLES, R), 1.0, 6.0, ((0, 8),), jnp.float32),
    }


BLOCK = 2048
RIDGE = 1.0


def block_masks(size, step, shift):
    cols = jnp.arange(F, dtype=jnp.int32)
    mult = 2 * step + 1
    coded = (cols[None, :] * mult[:, None] + shift[:, None]) % F
    return 2.0 * (coded < size[:, None]).astype(jnp.float32) - 1.0


def kernel_weights(size):
    kf = size.astype(jnp.float32)
    return (F * (F - 1)) / (kf * (F - kf) * SAMPLES)


def reference(coal_size, coal_step, coal_shift, outputs_y):
    nblk = SAMPLES // min(BLOCK, SAMPLES)
    rows = SAMPLES // nblk
    sizes = coal_size.reshape(nblk, rows)
    steps = coal_step.reshape(nblk, rows)
    shifts = coal_shift.reshape(nblk, rows)
    ys = outputs_y.reshape(nblk, rows, R)
    high = lax.Precision.HIGHEST

    def target_blk(carry, pieces):
        size, step, shift, yblk = pieces
        masks = block_masks(size, step, shift)
        scaled = kernel_weights(size)[:, None] * yblk
        return carry + jnp.dot(masks.T, scaled, precision=high, preferred_element_type=jnp.float32), None

    def operate(vec):
        def one_blk(carry, pieces):
            size, step, shift = pieces
            masks = block_masks(size, step, shift)
            values = jnp.dot(masks, vec, precision=high, preferred_element_type=jnp.float32)
            scaled = kernel_weights(size)[:, None] * values
            return carry + jnp.dot(masks.T, scaled, precision=high, preferred_element_type=jnp.float32), None
        total, _ = lax.scan(one_blk, jnp.zeros((F, R), jnp.float32), (sizes, steps, shifts))
        return total + RIDGE * vec

    target, _ = lax.scan(target_blk, jnp.zeros((F, R), jnp.float32), (sizes, steps, shifts, ys))
    attributions = jnp.zeros((F, R), jnp.float32)
    residual = target
    direction = target
    norm_now = jnp.sum(residual * residual, axis=0)
    for step in range(ITERS):
        image = operate(direction)
        alpha = norm_now / jnp.sum(direction * image, axis=0)
        attributions = attributions + alpha * direction
        residual = residual - alpha * image
        norm_next = jnp.sum(residual * residual, axis=0)
        direction = residual + (norm_next / norm_now) * direction
        norm_now = norm_next
    return attributions, residual
```

```python
import functools

import jax
import jax.numpy as jnp
from jax import lax
from jax.experimental import pallas as pl
from jax.experimental.pallas import tpu as pltpu
from jax.sharding import PartitionSpec as P

F = 4096
R = 32
ITERS = 2

RIDGE = 1.0
HIGH = lax.Precision.HIGHEST
LANES = 128
GRAM_LIMIT = 512
LOW = -(2 ** 31)


def contract_rows(left, right):
    return lax.dot_general(
        left, right, (((0,), (0,)), ((), ())), precision=HIGH, preferred_element_type=jnp.float32
    )


def body(coal_size, coal_step, coal_shift, outputs_y):
    n_smp = lax.axis_size("smp")
    n_feat = lax.axis_size("feat")
    half = F // n_feat
    share = half // n_smp
    samples = coal_size.shape[0] * n_smp
    feat_index = lax.axis_index("feat")
    local = jnp.arange(half, dtype=jnp.int32)
    columns = (local // share * n_feat + feat_index) * share + local % share
    mult = 2 * coal_step + 1
    coded = (columns[None, :] * mult[:, None] + coal_shift[:, None]) % F
    masks = 2.0 * (coded < coal_size[:, None]).astype(jnp.float32) - 1.0
    kf = coal_size.astype(jnp.float32)
    weights = F * (F - 1) / (kf * (F - kf) * samples)
    first = weights[:, None] * outputs_y

    def totals(scaled):
        return lax.psum(contract_rows(masks, scaled), "smp")

    def column_dots(product):
        return lax.psum(jnp.sum(product, axis=0), "feat")

    target = totals(first)
    attributions = jnp.zeros_like(target)
    residual = target
    direction = target
    norm_now = column_dots(residual * residual)
    for step in range(ITERS):
        part = jnp.dot(masks, direction, precision=HIGH, preferred_element_type=jnp.float32)
        image = totals(weights[:, None] * lax.psum(part, "feat")) + RIDGE * direction
        alpha = norm_now / column_dots(direction * image)
        attributions = attributions + alpha * direction
        residual = residual - alpha * image
        norm_next = column_dots(residual * residual)
        direction = residual + norm_next / norm_now * direction
        norm_now = norm_next
    offset = lax.axis_index("smp") * share
    attributions = lax.dynamic_slice_in_dim(attributions, offset, share, 0)
    residual = lax.dynamic_slice_in_dim(residual, offset, share, 0)
    return (attributions, residual)


def split(v):
    a = v.astype(jnp.bfloat16)
    v = v - a.astype(jnp.float32)
    b = v.astype(jnp.bfloat16)
    v = v - b.astype(jnp.float32)
    return jnp.concatenate([a, b, v.astype(jnp.bfloat16)], axis=0)


def join(v, rows):
    return v[:rows] + (v[rows:2 * rows] + v[2 * rows:])


def mm(a, b):
    return jnp.dot(a, b, preferred_element_type=jnp.float32)


def kernel(n, n_feat, size_ref, step_ref, shift_ref, y_ref, out_ref,
           coal, ys, masks, send_c, recv_c, send_y, recv_y):
    me = lax.axis_index("smp")
    own = size_ref.shape[1]
    samples = own * n
    share = F // (n * n_feat)

    coal[me, 0:1, 0:own] = size_ref[...].astype(jnp.float32)
    coal[me, 1:2, 0:own] = step_ref[...].astype(jnp.float32)
    coal[me, 2:3, 0:own] = shift_ref[...].astype(jnp.float32)
    yt = y_ref[...].T
    ys[me, :, 0:own] = yt[: R // 2]
    ys[me, :, own:2 * own] = yt[R // 2:]

    barrier = pltpu.get_barrier_semaphore()
    for k in range(1, n):
        pl.semaphore_signal(barrier, inc=1, device_id={"smp": lax.rem(me + k, n)})
    pl.semaphore_wait(barrier, n - 1)

    coal_copies, y_copies = [], []
    for k in range(1, n):
        copy = pltpu.make_async_remote_copy(
            src_ref=coal.at[me], dst_ref=coal.at[me], send_sem=send_c.at[k], recv_sem=recv_c.at[k],
            device_id={"smp": lax.rem(me + k, n)})
        copy.start()
        coal_copies.append(copy)
    for k in range(1, n):
        copy = pltpu.make_async_remote_copy(
            src_ref=ys.at[me], dst_ref=ys.at[me], send_sem=send_y.at[k], recv_sem=recv_y.at[k],
            device_id={"smp": lax.rem(me + k, n)})
        copy.start()
        y_copies.append(copy)

    lane = lax.broadcasted_iota(jnp.int32, (own, LANES), 1)
    one = jnp.full((own, LANES), 1.0, jnp.float32)
    for k in range(n):
        peer = lax.rem(me + n - k, n)
        if k:
            coal_copies[k - 1].wait_recv()
        cols = coal[peer].T[0:own].astype(jnp.int32)
        size = jnp.broadcast_to(cols[:, 0:1], (own, LANES))
        mult = 2 * jnp.broadcast_to(cols[:, 1:2], (own, LANES)) + 1
        shift = jnp.broadcast_to(cols[:, 2:3], (own, LANES))
        code = ((lane * mult + shift) << 20) + LOW
        limit = (size << 20) + LOW
        stride = mult << 27
        rows = pl.ds(pl.multiple_of(peer * own, own), own)
        for c in range(F // LANES):
            masks[rows, c * LANES:(c + 1) * LANES] = jnp.where(code < limit, one, -one).astype(masks.dtype)
            code = code + stride

    m = masks[...]
    gram = lax.dot_general(m, m, (((1,), (1,)), ((), ())), preferred_element_type=jnp.float32)
    gram_hi = gram.astype(jnp.bfloat16)
    gram_lo = (gram - gram_hi.astype(jnp.float32)).astype(jnp.bfloat16)

    def by_gram(v):
        s = split(v)
        return join(mm(s, gram_hi) + mm(s, gram_lo), R)

    left = lax.broadcasted_iota(jnp.int32, (R // 2, LANES), 1) < own
    kf, y = [], []
    for copy in y_copies:
        copy.wait_recv()
    for q in range(0, n, 2):
        t0, t1 = coal[q, 0:1], coal[q + 1, 0:1]
        kf.append(jnp.where(left[0:1], t0, pltpu.roll(t1, own, 1)))
        t0, t1 = ys[q], ys[q + 1]
        y.append(jnp.concatenate([
            jnp.where(left, t0, pltpu.roll(t1, own, 1)),
            jnp.where(left, pltpu.roll(t0, own, 1), t1)], axis=0))
    kf = jnp.concatenate(kf, axis=1)
    y = jnp.concatenate(y, axis=1)
    weights = F * (F - 1) / (kf * (F - kf) * samples)

    def dots(product):
        return jnp.sum(product, axis=1, keepdims=True)

    residual = weights * y
    direction = residual
    seen = by_gram(residual)
    norm_now = dots(residual * seen)
    attributions = jnp.zeros_like(residual)
    for step in range(ITERS):
        image = weights * seen + RIDGE * direction
        alpha = norm_now / dots(seen * image)
        attributions = attributions + alpha * direction
        residual = residual - alpha * image
        if step < ITERS - 1:
            fresh = by_gram(residual)
            norm_next = dots(residual * fresh)
            beta = norm_next / norm_now
            direction = residual + beta * direction
            seen = fresh + beta * seen
            norm_now = norm_next

    place = me * n_feat + lax.axis_index("feat")
    mine = masks[:, pl.ds(pl.multiple_of(place * share, share), share)]
    both = jnp.concatenate([attributions, residual], axis=0)
    out_ref[...] = join(mm(split(both), mine), 2 * R)
    for copy in coal_copies + y_copies:
        copy.wait_send()


def gram_body(n, n_feat, coal_size, coal_step, coal_shift, outputs_y):
    own = coal_size.shape[0]
    share = F // (n * n_feat)
    out = pl.pallas_call(
        functools.partial(kernel, n, n_feat),
        out_shape=jax.ShapeDtypeStruct((2 * R, share), jnp.float32),
        in_specs=[pl.BlockSpec(memory_space=pltpu.VMEM)] * 4,
        out_specs=pl.BlockSpec(memory_space=pltpu.VMEM),
        scratch_shapes=[
            pltpu.VMEM((n, 8, LANES), jnp.float32),
            pltpu.VMEM((n, R // 2, LANES), jnp.float32),
            pltpu.VMEM((own * n, F), jnp.bfloat16),
            pltpu.SemaphoreType.DMA((n,)),
            pltpu.SemaphoreType.DMA((n,)),
            pltpu.SemaphoreType.DMA((n,)),
            pltpu.SemaphoreType.DMA((n,)),
        ],
        compiler_params=pltpu.CompilerParams(collective_id=0, has_side_effects=True),
    )(coal_size.reshape(1, own), coal_step.reshape(1, own), coal_shift.reshape(1, own), outputs_y)
    return out[:R].T, out[R:].T


def solution(mesh):
    n, n_feat = mesh.shape["smp"], mesh.shape["feat"]

    def chosen(coal_size, coal_step, coal_shift, outputs_y):
        own = coal_size.shape[0]
        if own * n <= GRAM_LIMIT and 2 * own == LANES and n % 2 == 0:
            return gram_body(n, n_feat, coal_size, coal_step, coal_shift, outputs_y)
        return body(coal_size, coal_step, coal_shift, outputs_y)

    placed = (P(("grp", "smp")), P(("grp", "smp")), P(("grp", "smp")), P(("grp", "smp"), None))
    return jax.shard_map(
        chosen,
        mesh=mesh,
        in_specs=placed,
        out_specs=(P(("grp", "smp", "feat"), None), P(("grp", "smp", "feat"), None)),
        check_vma=False,
    )
```

```python
import functools

import jax
import jax.numpy as jnp
from jax import lax
from jax.experimental import pallas as pl
from jax.experimental.pallas import tpu as pltpu
from jax.sharding import PartitionSpec as P

F = 4096
R = 32
ITERS = 2

RIDGE = 1.0
HIGH = lax.Precision.HIGHEST
LANES = 128
GRAM_LIMIT = 512
LOW = -(2 ** 31)
CODES = 4
MASK_TYPE = jnp.float8_e4m3fn
VMEM_BYTES = 20 * 2 ** 20


def contract_rows(left, right):
    return lax.dot_general(
        left, right, (((0,), (0,)), ((), ())), precision=HIGH, preferred_element_type=jnp.float32
    )


def body(coal_size, coal_step, coal_shift, outputs_y):
    n_smp = lax.axis_size("smp")
    n_feat = lax.axis_size("feat")
    half = F // n_feat
    share = half // n_smp
    samples = coal_size.shape[0] * n_smp
    feat_index = lax.axis_index("feat")
    local = jnp.arange(half, dtype=jnp.int32)
    columns = (local // share * n_feat + feat_index) * share + local % share
    mult = 2 * coal_step + 1
    coded = (columns[None, :] * mult[:, None] + coal_shift[:, None]) % F
    masks = 2.0 * (coded < coal_size[:, None]).astype(jnp.float32) - 1.0
    kf = coal_size.astype(jnp.float32)
    weights = F * (F - 1) / (kf * (F - kf) * samples)
    first = weights[:, None] * outputs_y

    def totals(scaled):
        return lax.psum(contract_rows(masks, scaled), "smp")

    def column_dots(product):
        return lax.psum(jnp.sum(product, axis=0), "feat")

    target = totals(first)
    attributions = jnp.zeros_like(target)
    residual = target
    direction = target
    norm_now = column_dots(residual * residual)
    for step in range(ITERS):
        part = jnp.dot(masks, direction, precision=HIGH, preferred_element_type=jnp.float32)
        image = totals(weights[:, None] * lax.psum(part, "feat")) + RIDGE * direction
        alpha = norm_now / column_dots(direction * image)
        attributions = attributions + alpha * direction
        residual = residual - alpha * image
        norm_next = column_dots(residual * residual)
        direction = residual + norm_next / norm_now * direction
        norm_now = norm_next
    offset = lax.axis_index("smp") * share
    attributions = lax.dynamic_slice_in_dim(attributions, offset, share, 0)
    residual = lax.dynamic_slice_in_dim(residual, offset, share, 0)
    return (attributions, residual)


def split(v):
    a = v.astype(jnp.bfloat16)
    v = v - a.astype(jnp.float32)
    b = v.astype(jnp.bfloat16)
    v = v - b.astype(jnp.float32)
    return jnp.concatenate([a, b, v.astype(jnp.bfloat16)], axis=0)


def join(v, rows):
    return v[:rows] + (v[rows:2 * rows] + v[2 * rows:])


def mm_nt(a, b):
    return lax.dot_general(a, b, (((1,), (1,)), ((), ())), preferred_element_type=jnp.float32)


def mm(a, b):
    return jnp.dot(a, b, preferred_element_type=jnp.float32)


def kernel(n, n_feat, size_in, step_in, shift_in, y_in, out_ref,
           ints, y_own, coal, ys, masks, in_sem, send_c, recv_c, send_y, recv_y):
    me = lax.axis_index("smp")
    own = size_in.shape[1]
    samples = own * n
    share = F // (n * n_feat)
    h = n // 2
    top = samples // 2
    base = me // h * h
    targets = [base + lax.rem(me + k, h) for k in range(h)] + [h - base + lax.rem(me + k, h) for k in range(h)]

    barrier = pltpu.get_barrier_semaphore()
    for k in range(1, n):
        pl.semaphore_signal(barrier, inc=1, device_id={"smp": targets[k]})

    loads = [pltpu.make_async_copy(ref, ints.at[i], in_sem.at[i])
             for i, ref in enumerate((size_in, step_in, shift_in))]
    loads.append(pltpu.make_async_copy(y_in, y_own, in_sem.at[3]))
    for load in loads:
        load.start()
    for load in loads:
        load.wait()
    for i in range(3):
        coal[0, i:i + 1, 0:own] = ints[i].astype(jnp.float32)
    yt = y_own[...]
    ys[0, :, 0:own] = yt[: R // 2]
    ys[0, :, own:2 * own] = yt[R // 2:]

    lane = lax.broadcasted_iota(jnp.int32, (own, LANES), 1)
    one = jnp.full((own, LANES), 1.0, jnp.float32)

    def build(k):
        cols = coal[k].T[0:own].astype(jnp.int32)
        size = jnp.broadcast_to(cols[:, 0:1], (own, LANES))
        mult = 2 * jnp.broadcast_to(cols[:, 1:2], (own, LANES)) + 1
        shift = jnp.broadcast_to(cols[:, 2:3], (own, LANES))
        code = ((lane * mult + shift) << 20) + LOW
        limit = (size << 20) + LOW
        stride = mult << 27
        for c in range(F // LANES):
            masks[k * own:(k + 1) * own, c * LANES:(c + 1) * LANES] = (
                jnp.where(code < limit, one, -one).astype(masks.dtype))
            code = code + stride

    build(0)
    pl.semaphore_wait(barrier, n - 1)

    def send(buffer, k, rows, send_sem, recv_sem):
        copy = pltpu.make_async_remote_copy(
            src_ref=buffer.at[0, pl.ds(0, rows)], dst_ref=buffer.at[k, pl.ds(0, rows)],
            send_sem=send_sem.at[k], recv_sem=recv_sem.at[k], device_id={"smp": targets[k]})
        copy.start()
        return copy

    order = list(range(h, n)) + list(range(1, h))
    coal_copies = {k: send(coal, k, CODES, send_c, recv_c) for k in order}
    y_copies = {k: send(ys, k, R // 2, send_y, recv_y) for k in order}

    def halves(v):
        hi = v.astype(jnp.bfloat16)
        return hi, (v - hi.astype(jnp.float32)).astype(jnp.bfloat16)

    for k in range(1, h):
        coal_copies[k].wait_recv()
        build(k)
    near = masks[0:top]
    g00 = halves(mm_nt(near, near))
    for k in range(h, n):
        coal_copies[k].wait_recv()
        build(k)
    far = masks[top:samples]
    g01 = halves(mm_nt(masks[0:top], far))
    g11 = halves(mm_nt(far, far))

    def by_gram(v):
        s = split(v)
        s0, s1 = s[:, :top], s[:, top:]
        first = (mm(s0, g00[0]) + mm_nt(s1, g01[0])) + (mm(s0, g00[1]) + mm_nt(s1, g01[1]))
        second = (mm(s0, g01[0]) + mm(s1, g11[0])) + (mm(s0, g01[1]) + mm(s1, g11[1]))
        return join(jnp.concatenate([first, second], axis=1), R)

    left = lax.broadcasted_iota(jnp.int32, (R // 2, LANES), 1) < own
    kf, y = [], []
    for k in order:
        y_copies[k].wait_recv()
    for q in range(0, n, 2):
        t0, t1 = coal[q, 0:1], coal[q + 1, 0:1]
        kf.append(jnp.where(left[0:1], t0, pltpu.roll(t1, own, 1)))
        t0, t1 = ys[q], ys[q + 1]
        y.append(jnp.concatenate([
            jnp.where(left, t0, pltpu.roll(t1, own, 1)),
            jnp.where(left, pltpu.roll(t0, own, 1), t1)], axis=0))
    kf = jnp.concatenate(kf, axis=1)
    y = jnp.concatenate(y, axis=1)
    weights = F * (F - 1) / (kf * (F - kf) * samples)

    def dots(product):
        return jnp.sum(product, axis=1, keepdims=True)

    residual = weights * y
    direction = residual
    seen = by_gram(residual)
    norm_now = dots(residual * seen)
    attributions = jnp.zeros_like(residual)
    for step in range(ITERS):
        image = weights * seen + RIDGE * direction
        alpha = norm_now / dots(seen * image)
        attributions = attributions + alpha * direction
        residual = residual - alpha * image
        if step < ITERS - 1:
            fresh = by_gram(residual)
            norm_next = dots(residual * fresh)
            beta = norm_next / norm_now
            direction = residual + beta * direction
            seen = fresh + beta * seen
            norm_now = norm_next

    place = me * n_feat + lax.axis_index("feat")
    mine = masks[:, pl.ds(pl.multiple_of(place * share, share), share)].astype(jnp.bfloat16)
    both = jnp.concatenate([attributions, residual], axis=0)
    out_ref[...] = join(mm(split(both), mine), 2 * R)
    for k in order:
        coal_copies[k].wait_send()
        y_copies[k].wait_send()


def gram_body(n, n_feat, coal_size, coal_step, coal_shift, outputs_y):
    own = coal_size.shape[0]
    share = F // (n * n_feat)
    out = pl.pallas_call(
        functools.partial(kernel, n, n_feat),
        out_shape=jax.ShapeDtypeStruct((2 * R, share), jnp.float32),
        in_specs=[pl.BlockSpec(memory_space=pltpu.HBM)] * 4,
        out_specs=pl.BlockSpec(memory_space=pltpu.VMEM),
        scratch_shapes=[
            pltpu.VMEM((3, 1, own), jnp.int32),
            pltpu.VMEM((R, own), jnp.float32),
            pltpu.VMEM((n, 8, LANES), jnp.float32),
            pltpu.VMEM((n, R // 2, LANES), jnp.float32),
            pltpu.VMEM((own * n, F), MASK_TYPE),
            pltpu.SemaphoreType.DMA((4,)),
            pltpu.SemaphoreType.DMA((n,)),
            pltpu.SemaphoreType.DMA((n,)),
            pltpu.SemaphoreType.DMA((n,)),
            pltpu.SemaphoreType.DMA((n,)),
        ],
        compiler_params=pltpu.CompilerParams(
            collective_id=0, has_side_effects=True, vmem_limit_bytes=VMEM_BYTES),
    )(coal_size.reshape(1, own), coal_step.reshape(1, own), coal_shift.reshape(1, own), outputs_y.T)
    return out[:R].T, out[R:].T


def solution(mesh):
    n, n_feat = mesh.shape["smp"], mesh.shape["feat"]

    def chosen(coal_size, coal_step, coal_shift, outputs_y):
        own = coal_size.shape[0]
        if own * n <= GRAM_LIMIT and 2 * own == LANES and n % 2 == 0:
            return gram_body(n, n_feat, coal_size, coal_step, coal_shift, outputs_y)
        return body(coal_size, coal_step, coal_shift, outputs_y)

    placed = (P(("grp", "smp")), P(("grp", "smp")), P(("grp", "smp")), P(("grp", "smp"), None))
    return jax.shard_map(
        chosen,
        mesh=mesh,
        in_specs=placed,
        out_specs=(P(("grp", "smp", "feat"), None), P(("grp", "smp", "feat"), None)),
        check_vma=False,
    )
```
